512 devices in a mesh: sub: 32 (over z_hi, x, core), lev: 16 (over y, z_lo).
Axes of the slice: x: 4, y: 4, z: 16 (z_hi: 4, z_lo: 4; z = z_hi * 4 + z_lo), core: 2. Of those that a mesh axis runs over, the one named last changes fastest.
Arguments:
- increment: float32 [6, 128, 64, 4096], P(None, 'lev', None, 'sub'), may hold values from -6 to 6
- std_dev: float32 [6, 128], P(None, 'lev'), may hold values from 0.5 to 2
- land_mask: int32 [64, 4096], P(None, 'sub'), may hold values 0 or 1
- row_class: int32 [64], replicated, may hold values from 0 to 7
- column_class: int32 [4096], P('sub'), may hold values from 0 to 7
- vertical_modes: float32 [6, 128, 128], replicated, as said below
- mode_variance: float32 [6, 128], replicated, may hold values from 0.25 to 4
Outputs:
- covaried: float32 [6, 128, 64, 4096], P(None, 'lev', None, 'sub')
The draws below stay inside these ranges and needn't reach their ends.
Inputs may be any that keep to these rules, and one draw needn't show every extreme that they name: `vertical_modes`: each variable's matrix is the identity plus independent entries of deviation 0.5 / sqrt(128).
All inputs are finite; a program needn't handle non-finite values. No bound on the sum of `land_mask` on one device may be relied on, other than what follows from the above.
Results may differ from the reference program's by a relative error of at most 0.0003.
Values sent between devices are 32-bit elements; how exact they have to be, the bound alone decides.
A program may use at most 64 MiB of HBM per device.

```python
import math
import jax
import jax.numpy as jnp
from jax import lax

VARS = 6
LEV = 128
MODES = 128
NY = 64
NX = 4096


def draw_vertical_modes(key, part):
    noise = jax.random.normal(key, (VARS, LEV, MODES), jnp.float32)
    identity_part = jnp.eye(LEV, MODES, dtype=jnp.float32)[None]
    return identity_part + 0.5 / math.sqrt(LEV) * noise


def plant(values, rng, smallest, largest):
    index_at = [jax.random.randint(jax.random.fold_in(rng, axis), (), 0, length) for axis, length in enumerate(values.shape)]
    widest = values.shape.index(max(values.shape))
    neighbour = index_at[:widest] + [(index_at[widest] + 1) % values.shape[widest]] + index_at[widest + 1:]
    return values.at[tuple(index_at)].set(smallest).at[tuple(neighbour)].set(largest)


def levels(stream_key, shape, split, least, high):
    gain, own = 1.0, jax.random.fold_in(stream_key, 6)
    for axis_at, shards_of in split:
        steps = jnp.exp(jax.random.uniform(jax.random.fold_in(own, axis_at), (shards_of,), jnp.float32, least / len(split), high / len(split)))
        gain = gain * jnp.repeat(steps, shape[axis_at] // shards_of).reshape([-1 if axis == axis_at else 1 for axis in range(len(shape))])
    return gain


def scatter_about(stream_key, dims, scale, reach, pieces=(), kind=jnp.bfloat16):
    values = jax.random.normal(stream_key, dims, jnp.float32) * scale
    if len(pieces) > 0:
        values = levels(stream_key, dims, pieces, -0.22, 0.18) * values
    return jnp.clip(values, min=-reach, max=reach).astype(kind)


def setup_inputs(seed: int = 0) -> dict:
    key_of = jax.random.split(jax.random.key(seed), 8)
    return {
        "increment": scatter_about(key_of[0], (VARS, LEV, NY, NX), 1.0, 6.0, ((1, 16), (3, 32)), jnp.float32),
        "std_dev": jnp.clip(jnp.exp(math.log(2.0) - 1.3862944 * jax.random.uniform(key_of[1], (VARS, LEV), jnp.float32) ** levels(key_of[1], (VARS, LEV), ((1, 16),), -0.2, 0.2)), 0.5, 2.0),
        "land_mask": plant((jax.random.randint(key_of[2], (NY, NX), 0, 3) < 1).astype(jnp.int32), jax.random.fold_in(key_of[2], 1), 0, 1),
        "row_class": plant(jax.random.randint(key_of[3], (NY,), 0, 8), jax.random.fold_in(key_of[3], 1), 0, 7).astype(jnp.int32),
        "column_class": plant(jax.random.randint(key_of[4], (NX,), 0, 8), jax.random.fold_in(key_of[4], 1), 0, 7).astype(jnp.int32),
        "vertical_modes": draw_vertical_modes(jax.random.fold_in(key_of[7], 71), 0),
        "mode_variance": jnp.clip(jnp.exp(jax.random.uniform(key_of[6], (VARS, MODES), jnp.float32, math.log(0.25), math.log(4.0))), 0.25, 4.0),
    }


def rate_table(length, fast_one, fast_two):
    return jnp.array([fast_one, fast_two, 0.3 / length, 0.6 / length, 1.0 / length, 1.4 / length, 1.8 / length, 2.2 / length], jnp.float32)

def recursion(stacked, decays, reverse):
    scaling = jnp.sqrt(1.0 - decays * decays)

    def advance(carried, column_in):
        carried = decays * carried + scaling * column_in
        return (carried, carried)
    start_state = jnp.zeros(stacked.shape[1:], stacked.dtype)
    _, history = lax.scan(advance, start_state, stacked, reverse=reverse)
    return history

def along_x(state, decays, reverse):
    return jnp.moveaxis(recursion(jnp.moveaxis(state, 3, 0), decays, reverse), 0, 3)

def along_y(state, decays, reverse):
    return jnp.moveaxis(recursion(jnp.moveaxis(state, 2, 0), decays, reverse), 0, 2)

def reference(increment, std_dev, land_mask, row_class, column_class, vertical_modes, mode_variance):
    decay_rows = jnp.exp(-rate_table(NX, 1.0 / 24, 1.0 / 40))[row_class]
    decay_cols = jnp.exp(-rate_table(NY, 1.0 / 8, 1.0 / 12))[column_class]
    weights = std_dev[:, :, None, None] * (1.0 + 0.8 * land_mask.astype(jnp.float32))[None, None]
    state = weights * increment
    state = along_x(state, decay_rows, True)
    state = along_y(state, decay_cols, True)
    amplitude = jnp.einsum('vlm,vlyx->vmyx', vertical_modes, state, precision=lax.Precision.HIGHEST)
    amplitude = amplitude * mode_variance[:, :, None, None]
    state = jnp.einsum('vlm,vmyx->vlyx', vertical_modes, amplitude, precision=lax.Precision.HIGHEST)
    state = along_y(state, decay_cols, False)
    state = along_x(state, decay_rows, False)
    return weights * state
```

```python
import jax
import jax.numpy as jnp
from jax import lax
from jax.sharding import PartitionSpec as P


def rate_table(length, fast_one, fast_two):
    return jnp.array(
        [
            fast_one,
            fast_two,
            0.3 / length,
            0.6 / length,
            1.0 / length,
            1.4 / length,
            1.8 / length,
            2.2 / length,
        ],
        jnp.float32,
    )


def decay_lookup(classes, rates):
    matches = classes[:, None] == jnp.arange(8, dtype=jnp.int32)[None, :]
    return jnp.sum(jnp.where(matches, jnp.exp(-rates)[None, :], 0.0), axis=1)


def filter_rows(decays, length):
    position = jnp.arange(length)
    distance = jnp.maximum(position[:, None] - position[None, :], 0).astype(jnp.float32)
    log_decay = jnp.log(decays)
    scaling = jnp.sqrt(1.0 - decays * decays)
    kernel = jnp.exp(distance[None] * log_decay[:, None, None]) * scaling[:, None, None]
    return jnp.where((position[:, None] >= position[None, :])[None], kernel, 0.0)


def carry_in(log_decay, span, outgoing, backward):
    devices = lax.axis_size("sub")
    me = lax.axis_index("sub")
    gathered = lax.all_gather(outgoing, "sub")
    others = jnp.arange(devices)
    gap = (others - me if backward else me - others) - 1
    reach = jnp.maximum(gap, 0).astype(jnp.float32) * span
    factors = jnp.where(
        (gap >= 0)[:, None], jnp.exp(reach[:, None] * log_decay[None, :]), 0.0
    )
    return jnp.sum(gathered * factors[:, None, None, :], axis=0)


def sweep_along(grid_field, decays, backward):
    span_x = grid_field.shape[3]
    kernel = filter_rows(decays, span_x)
    log_decay = jnp.log(decays)
    position = jnp.arange(span_x, dtype=jnp.float32)
    if backward:
        inside = jnp.einsum("vlyi,yij->vlyj", grid_field, kernel, precision=lax.Precision.HIGHEST)
        outgoing = inside[..., 0]
        decays_in = jnp.exp((span_x - position)[None, :] * log_decay[:, None])
    else:
        inside = jnp.einsum("vlyj,yij->vlyi", grid_field, kernel, precision=lax.Precision.HIGHEST)
        outgoing = inside[..., span_x - 1]
        decays_in = jnp.exp((position + 1.0)[None, :] * log_decay[:, None])
    incoming = carry_in(log_decay, span_x, outgoing, backward)
    return inside + incoming[..., None] * decays_in[None, None]


def project_modes(level_slab, vertical_modes, mode_variance):
    amplitude = jnp.einsum(
        "vlm,vlrc->vmrc", vertical_modes, level_slab, precision=lax.Precision.HIGHEST
    )
    amplitude = amplitude * mode_variance[:, :, None, None]
    return jnp.einsum("vlm,vmrc->vlrc", vertical_modes, amplitude, precision=lax.Precision.HIGHEST)


def on_device(
    increment, std_dev, land_mask, row_class, column_class, vertical_modes, mode_variance
):
    row_count = increment.shape[2]
    total_x = increment.shape[3] * lax.axis_size("sub")
    decay_rows = decay_lookup(row_class, rate_table(total_x, 1.0 / 24, 1.0 / 40))
    decay_cols = decay_lookup(column_class, rate_table(row_count, 1.0 / 8, 1.0 / 12))
    kernel_cols = filter_rows(decay_cols, row_count)
    weights = std_dev[:, :, None, None] * (1.0 + 0.8 * land_mask.astype(jnp.float32))[None, None]
    state = weights * increment
    state = sweep_along(state, decay_rows, True)
    state = jnp.einsum("vlix,xij->vljx", state, kernel_cols, precision=lax.Precision.HIGHEST)
    mixed = project_modes(
        lax.all_to_all(state, "lev", split_axis=2, concat_axis=1, tiled=True),
        vertical_modes,
        mode_variance,
    )
    state = lax.all_to_all(mixed, "lev", split_axis=1, concat_axis=2, tiled=True)
    state = jnp.einsum("vljx,xij->vlix", state, kernel_cols, precision=lax.Precision.HIGHEST)
    state = sweep_along(state, decay_rows, False)
    return weights * state


def solution(mesh):
    return jax.shard_map(
        on_device,
        mesh=mesh,
        in_specs=(
            P(None, "lev", None, "sub"),
            P(None, "lev"),
            P(None, "sub"),
            P(),
            P("sub"),
            P(),
            P(),
        ),
        out_specs=P(None, "lev", None, "sub"),
        check_vma=False,
    )
```

```python
import functools

import jax
import jax.numpy as jnp
from jax import lax
from jax.experimental import pallas as pl
from jax.experimental.pallas import tpu as pltpu
from jax.sharding import PartitionSpec as P

MESH = pl.DeviceIdType.MESH
HALF = 3
NEAR = 8


def rate_table(length, fast_one, fast_two):
    return jnp.array(
        [
            fast_one,
            fast_two,
            0.3 / length,
            0.6 / length,
            1.0 / length,
            1.4 / length,
            1.8 / length,
            2.2 / length,
        ],
        jnp.float32,
    )


def decay_lookup(classes, rates):
    matches = classes[:, None] == jnp.arange(8, dtype=jnp.int32)[None, :]
    return jnp.sum(jnp.where(matches, jnp.exp(-rates)[None, :], 0.0), axis=1)


def tables_along_x(decays, span, blocks):
    lane = jnp.arange(span)
    log_decay = jnp.log(decays)
    powers, doubling = decays, []
    for k in range(span.bit_length() - 1):
        doubling.append(powers)
        powers = powers * powers
    offsets = 2 ** jnp.arange(len(doubling))
    doubling = jnp.stack(doubling, axis=1)[:, :, None]
    ahead = (lane[None, :] + offsets[:, None] < span)[None]
    behind = (lane[None, :] >= offsets[:, None])[None]
    entering_b = jnp.exp((span - lane).astype(jnp.float32)[None] * log_decay[:, None])
    entering_f = jnp.exp((lane + 1).astype(jnp.float32)[None] * log_decay[:, None])
    steps_b = jnp.concatenate([jnp.where(ahead, doubling, 0.0), entering_b[:, None]], axis=1)
    steps_f = jnp.concatenate([jnp.where(behind, doubling, 0.0), entering_f[:, None]], axis=1)

    me = lax.axis_index("sub")
    mine, block = me % NEAR, me // NEAR
    near, far = jnp.arange(NEAR), jnp.arange(blocks)

    def power(gap):
        reach = jnp.maximum(gap, 0).astype(jnp.float32) * span
        grown = jnp.exp(reach[:, None] * log_decay[None])
        return jnp.where((gap >= 0)[:, None], grown, 0.0)

    def gated(keep, gap):
        return jnp.where(keep[:, None], power(gap), 0.0)

    mix = jnp.concatenate(
        [
            power(near - mine - 1),
            power(near),
            gated(far > block, NEAR * (far - block - 1) + NEAR - 1 - mine),
            power(mine - near - 1),
            power(NEAR - 1 - near),
            gated(far < block, NEAR * (block - far - 1) + mine),
        ]
    )
    return steps_b, steps_f, jnp.pad(mix, ((0, 0), (0, span - mix.shape[1])))


def kernel(
    subs,
    levs,
    field_ref,
    std_ref,
    land_ref,
    gain_ref,
    steps_b_ref,
    steps_f_ref,
    mix_ref,
    cols_ref,
    modes_ref,
    variance_ref,
    out_ref,
    slab,
    gathered,
    mixed,
    returned,
    work,
    packed,
    near_in,
    block_sum,
    far_in,
    matrix,
    in_send,
    in_recv,
    out_send,
    out_recv,
    near_send,
    near_recv,
    far_send,
    far_recv,
):
    sub, lev = lax.axis_index("sub"), lax.axis_index("lev")
    mine, block = sub % NEAR, sub // NEAR
    blocks = subs // NEAR
    rows = land_ref.shape[0]
    span = land_ref.shape[1]
    share = rows // levs
    tall = slab.shape[2]
    doublings = span.bit_length() - 1
    lanes = lax.broadcasted_iota(jnp.int32, (tall, span), 1)

    def lev_peer(k):
        return (lev + k) % levs

    def near_peer(k):
        return block * NEAR + (mine + k) % NEAR

    def far_peer(k):
        return ((block + k) % blocks) * NEAR + mine

    barrier = pltpu.get_barrier_semaphore()

    @pl.loop(1, levs)
    def _(k):
        pl.semaphore_signal(barrier, inc=1, device_id=(sub, lev_peer(k)), device_id_type=MESH)

    @pl.loop(1, NEAR)
    def _(k):
        pl.semaphore_signal(barrier, inc=1, device_id=(near_peer(k), lev), device_id_type=MESH)

    @pl.loop(1, blocks)
    def _(k):
        pl.semaphore_signal(barrier, inc=1, device_id=(far_peer(k), lev), device_id_type=MESH)

    def weight(half, y):
        return std_ref[pl.ds(half * tall, tall), :] * land_ref[pl.ds(y, 1), :]

    def natural(half, y):
        return pl.ds(half * tall * rows + y, tall, stride=rows)

    def load_weighted(half, y):
        return field_ref[natural(half, y), :] * weight(half, y)

    def remote(src, dst, send, recv, target):
        return pltpu.make_async_remote_copy(
            src_ref=src, dst_ref=dst, send_sem=send, recv_sem=recv,
            device_id=target, device_id_type=MESH,
        )

    def whole(ref, sem):
        pltpu.make_async_copy(ref, ref, sem).wait()

    def lanes_of(v):
        return pl.ds(v * 8, 8)

    def send_levels(half, v):
        def part(peer):
            return slab.at[half, pl.ds(peer * share, share), lanes_of(v), :]

        place = gathered.at[half, v, :, pl.ds(lev * 8, 8), :]

        @pl.loop(1, levs)
        def _(k):
            peer = lev_peer(k)
            remote(part(peer), place, in_send.at[half, v], in_recv.at[half, v], (sub, peer)).start()

        pltpu.make_async_copy(part(lev), place, in_recv.at[half, v]).start()

    def send_back(half, v):
        def part(peer):
            return mixed.at[half, v, :, pl.ds(peer * 8, 8), :]

        place = returned.at[half, pl.ds(lev * share, share), lanes_of(v), :]

        @pl.loop(1, levs)
        def _(k):
            peer = lev_peer(k)
            remote(part(peer), place, out_send.at[half, v], out_recv.at[half, v], (sub, peer)).start()

        pltpu.make_async_copy(part(lev), place, out_recv.at[half, v]).start()

    def make_matrix(var):
        modes = modes_ref[var]
        product = lax.dot_general(
            modes * variance_ref[var], modes, (((1,), (1,)), ((), ())),
            precision=lax.Precision.HIGHEST, preferred_element_type=jnp.float32,
        )
        high = product.astype(jnp.bfloat16)
        matrix[var, :, : high.shape[1]] = high
        matrix[var, :, high.shape[1] :] = (product - high.astype(jnp.float32)).astype(jnp.bfloat16)

    def mix_levels(half, v):
        whole(gathered.at[half, v], in_recv.at[half, v])
        both = matrix[half * HALF + v]
        high_part = both[:, : both.shape[1] // 2]
        for r in range(share):
            value = gathered[half, v, r]
            high = value.astype(jnp.bfloat16)
            low = (value - high.astype(jnp.float32)).astype(jnp.bfloat16)
            mixed[half, v, r] = jnp.dot(
                both, jnp.concatenate([high, high], axis=0), preferred_element_type=jnp.float32
            ) + jnp.dot(high_part, low, preferred_element_type=jnp.float32)
        send_back(half, v)

    def doubled(value, steps, y, backward):
        for k in range(doublings):
            shift = span - 2**k if backward else 2**k
            value = value + steps[y, k : k + 1, :] * pltpu.roll(value, shift, 1)
        return value

    def send_near(half, way):
        place = near_in.at[half, way, mine]

        @pl.loop(1, NEAR)
        def _(k):
            remote(
                packed.at[half, way], place, near_send.at[half, way],
                near_recv.at[half, way], (near_peer(k), lev),
            ).start()

        pltpu.make_async_copy(packed.at[half, way], place, near_recv.at[half, way]).start()

    def factor(way, row):
        return mix_ref[pl.ds(way * (2 * NEAR + blocks) + row, 1), :]

    def send_far(half, way):
        whole(near_in.at[half, way], near_recv.at[half, way])
        total = jnp.zeros((tall, span), jnp.float32)
        for j in range(NEAR):
            total = total + factor(way, NEAR + j) * near_in[half, way, j]
        block_sum[half, way] = total
        place = far_in.at[half, way, block]

        @pl.loop(1, blocks)
        def _(k):
            remote(
                block_sum.at[half, way], place, far_send.at[half, way],
                far_recv.at[half, way], (far_peer(k), lev),
            ).start()

        pltpu.make_async_copy(block_sum.at[half, way], place, far_recv.at[half, way]).start()

    def incoming(half, way):
        total = jnp.zeros((tall, span), jnp.float32)
        for j in range(NEAR):
            total = total + factor(way, j) * near_in[half, way, j]
        whole(far_in.at[half, way], far_recv.at[half, way])
        for j in range(blocks):
            total = total + factor(way, 2 * NEAR + j) * far_in[half, way, j]
        return total

    def spread(state, y):
        return jnp.broadcast_to(pltpu.roll(state, (span - y) % span, 1)[:, 0:1], (tall, span))

    together = 4

    def first_sweep(half, load):
        def body(i, pack):
            for u in range(together):
                y = i * together + u
                value = doubled(load(y) * gain_ref[pl.ds(y, 1), :], steps_b_ref, y, True)
                work[half, y] = value
                pack = jnp.where(lanes == y, pltpu.roll(value, y, 1), pack)
            return pack

        packed[half, 0] = lax.fori_loop(
            0, rows // together, body, jnp.zeros((tall, span), jnp.float32)
        )
        send_near(half, 0)

    def second_sweep(half):
        state = incoming(half, 0)
        decay, scaling = cols_ref[0:1, :], cols_ref[1:2, :]

        def down(i, carried):
            for u in range(together):
                y = rows - 1 - (i * together + u)
                entered = work[half, y] + steps_b_ref[y, doublings : doublings + 1, :] * spread(state, y)
                carried = decay * carried + scaling * entered
                work[half, y] = carried
            return carried

        zero = jnp.zeros((tall, span), jnp.float32)
        lax.fori_loop(0, rows // together, down, zero)

        def up(i, both):
            carried, pack = both
            for u in range(together):
                y = i * together + u
                carried = decay * carried + scaling * work[half, y]
                value = doubled(carried * gain_ref[pl.ds(y, 1), :], steps_f_ref, y, False)
                work[half, y] = value
                pack = jnp.where(lanes == y, pltpu.roll(value, y + 1, 1), pack)
            return carried, pack

        packed[half, 1] = lax.fori_loop(0, rows // together, up, (zero, zero))[1]
        send_near(half, 1)

    def last_sweep(half, store):
        state = incoming(half, 1)

        @pl.loop(0, rows // together)
        def _(i):
            for u in range(together):
                y = i * together + u
                store(y, work[half, y] + steps_f_ref[y, doublings : doublings + 1, :] * spread(state, y))

    @pl.loop(0, rows // together)
    def _(i):
        for u in range(together):
            y = i * together + u
            slab[0, y] = load_weighted(0, y)

    pl.semaphore_wait(barrier, levs + NEAR + blocks - 3)

    for v in range(HALF):
        send_levels(0, v)
    first_sweep(1, lambda y: load_weighted(1, y))

    @pl.loop(0, 2 * HALF)
    def _(var):
        make_matrix(var)

    send_far(1, 0)
    mix_levels(0, 0)
    second_sweep(1)
    mix_levels(0, 1)
    send_far(1, 1)
    mix_levels(0, 2)

    def to_slab(y, value):
        slab[1, y] = value

    last_sweep(1, to_slab)
    for v in range(HALF):
        send_levels(1, v)

    for v in range(HALF):
        whole(returned.at[0, :, lanes_of(v), :], out_recv.at[0, v])
    first_sweep(0, lambda y: returned[0, y])
    mix_levels(1, 0)
    send_far(0, 0)
    mix_levels(1, 1)
    second_sweep(0)
    mix_levels(1, 2)
    send_far(0, 1)

    def to_output(y, value):
        out_ref[natural(0, y), :] = value * weight(0, y)

    last_sweep(0, to_output)

    for v in range(HALF):
        whole(returned.at[1, :, lanes_of(v), :], out_recv.at[1, v])

    @pl.loop(0, rows // together)
    def _(i):
        for u in range(together):
            y = i * together + u
            out_ref[natural(1, y), :] = returned[1, y] * weight(1, y)

    for half in range(2):
        for v in range(HALF):
            sent = gathered.at[half, v, :, pl.ds(0, (levs - 1) * 8), :]
            whole(sent, in_send.at[half, v])
            whole(sent, out_send.at[half, v])
        for way in range(2):
            whole(near_in.at[half, way, pl.ds(0, NEAR - 1)], near_send.at[half, way])
            whole(far_in.at[half, way, pl.ds(0, blocks - 1)], far_send.at[half, way])


def on_device(
    increment, std_dev, land_mask, row_class, column_class, vertical_modes, mode_variance
):
    variables, levels, rows, span = increment.shape
    subs, levs = lax.axis_size("sub"), lax.axis_size("lev")
    blocks = subs // NEAR
    decay_rows = decay_lookup(row_class, rate_table(span * subs, 1.0 / 24, 1.0 / 40))
    decay_cols = decay_lookup(column_class, rate_table(rows, 1.0 / 8, 1.0 / 12))
    gain_rows = jnp.sqrt(1.0 - decay_rows * decay_rows)
    gain_cols = jnp.sqrt(1.0 - decay_cols * decay_cols)
    steps_b, steps_f, mix = tables_along_x(decay_rows, span, blocks)
    tall = HALF * levels
    deep = levels * levs
    share = rows // levs
    f32 = jnp.float32
    result = pl.pallas_call(
        functools.partial(kernel, subs, levs),
        out_shape=jax.ShapeDtypeStruct((variables * levels * rows, span), f32),
        in_specs=[pl.BlockSpec(memory_space=pltpu.VMEM)] * 10,
        out_specs=pl.BlockSpec(memory_space=pltpu.VMEM),
        scratch_shapes=[
            pltpu.VMEM((2, rows, tall, span), f32),
            pltpu.VMEM((2, HALF, share, deep, span), f32),
            pltpu.VMEM((2, HALF, share, deep, span), f32),
            pltpu.VMEM((2, rows, tall, span), f32),
            pltpu.VMEM((2, rows, tall, span), f32),
            pltpu.VMEM((2, 2, tall, span), f32),
            pltpu.VMEM((2, 2, NEAR, tall, span), f32),
            pltpu.VMEM((2, 2, tall, span), f32),
            pltpu.VMEM((2, 2, blocks, tall, span), f32),
            pltpu.VMEM((variables, deep, 2 * deep), jnp.bfloat16),
            pltpu.SemaphoreType.DMA((2, HALF)),
            pltpu.SemaphoreType.DMA((2, HALF)),
            pltpu.SemaphoreType.DMA((2, HALF)),
            pltpu.SemaphoreType.DMA((2, HALF)),
            pltpu.SemaphoreType.DMA((2, 2)),
            pltpu.SemaphoreType.DMA((2, 2)),
            pltpu.SemaphoreType.DMA((2, 2)),
            pltpu.SemaphoreType.DMA((2, 2)),
        ],
        compiler_params=pltpu.CompilerParams(
            collective_id=0, has_side_effects=True, vmem_limit_bytes=40 * 2**20
        ),
    )(
        increment.reshape(variables * levels * rows, span),
        jnp.broadcast_to(std_dev.reshape(variables * levels, 1), (variables * levels, span)),
        1.0 + 0.8 * land_mask.astype(f32),
        jnp.broadcast_to(gain_rows[:, None], (rows, span)),
        steps_b,
        steps_f,
        mix,
        jnp.stack([decay_cols, gain_cols]),
        vertical_modes,
        mode_variance[:, None, :],
    )
    return result.reshape(increment.shape)


def solution(mesh):
    return jax.shard_map(
        on_device,
        mesh=mesh,
        in_specs=(
            P(None, "lev", None, "sub"),
            P(None, "lev"),
            P(None, "sub"),
            P(),
            P("sub"),
            P(),
            P(),
        ),
        out_specs=P(None, "lev", None, "sub"),
        check_vma=False,
    )
```

```python
import functools

import jax
import jax.numpy as jnp
from jax import lax
from jax.experimental import pallas as pl
from jax.experimental.pallas import tpu as pltpu
from jax.sharding import PartitionSpec as P

MESH = pl.DeviceIdType.MESH
HALF = 3
NEAR = 8


def rate_table(length, fast_one, fast_two):
    return jnp.array(
        [
            fast_one,
            fast_two,
            0.3 / length,
            0.6 / length,
            1.0 / length,
            1.4 / length,
            1.8 / length,
            2.2 / length,
        ],
        jnp.float32,
    )


def decay_lookup(classes, rates):
    matches = classes[:, None] == jnp.arange(8, dtype=jnp.int32)[None, :]
    return jnp.sum(jnp.where(matches, jnp.exp(-rates)[None, :], 0.0), axis=1)


def tables_along_x(decays, span, blocks):
    lane = jnp.arange(span)
    log_decay = jnp.log(decays)
    powers, doubling = decays, []
    for k in range(span.bit_length() - 1):
        doubling.append(powers)
        powers = powers * powers
    offsets = 2 ** jnp.arange(len(doubling))
    doubling = jnp.stack(doubling, axis=1)[:, :, None]
    ahead = (lane[None, :] + offsets[:, None] < span)[None]
    behind = (lane[None, :] >= offsets[:, None])[None]
    entering_b = jnp.exp((span - lane).astype(jnp.float32)[None] * log_decay[:, None])
    entering_f = jnp.exp((lane + 1).astype(jnp.float32)[None] * log_decay[:, None])
    steps_b = jnp.concatenate([jnp.where(ahead, doubling, 0.0), entering_b[:, None]], axis=1)
    steps_f = jnp.concatenate([jnp.where(behind, doubling, 0.0), entering_f[:, None]], axis=1)

    me = lax.axis_index("sub")
    mine, block = me % NEAR, me // NEAR
    near, far = jnp.arange(NEAR), jnp.arange(blocks)

    def power(gap):
        reach = jnp.maximum(gap, 0).astype(jnp.float32) * span
        grown = jnp.exp(reach[:, None] * log_decay[None])
        return jnp.where((gap >= 0)[:, None], grown, 0.0)

    def gated(keep, gap):
        return jnp.where(keep[:, None], power(gap), 0.0)

    mix = jnp.concatenate(
        [
            power(near - mine - 1),
            power(near),
            gated(far > block, NEAR * (far - block - 1) + NEAR - 1 - mine),
            power(mine - near - 1),
            power(NEAR - 1 - near),
            gated(far < block, NEAR * (block - far - 1) + mine),
        ]
    )
    return steps_b, steps_f, jnp.pad(mix, ((0, 0), (0, span - mix.shape[1])))


def kernel(
    subs,
    levs,
    field_ref,
    std_ref,
    land_ref,
    gain_ref,
    steps_b_ref,
    steps_f_ref,
    mix_ref,
    cols_ref,
    modes_ref,
    variance_ref,
    out_ref,
    slab,
    gathered,
    mixed,
    returned,
    work,
    packed,
    near_in,
    block_sum,
    far_in,
    matrix,
    in_send,
    in_recv,
    out_send,
    out_recv,
    near_send,
    near_recv,
    far_send,
    far_recv,
):
    sub, lev = lax.axis_index("sub"), lax.axis_index("lev")
    mine, block = sub % NEAR, sub // NEAR
    blocks = subs // NEAR
    rows = land_ref.shape[0]
    span = land_ref.shape[1]
    share = rows // levs
    tall = work.shape[2]
    deep = matrix.shape[1]
    doublings = span.bit_length() - 1
    lanes = lax.broadcasted_iota(jnp.int32, (tall, span), 1)

    wide = levs // 4

    def lev_peer(k):
        order = (k - 1) // 2
        far = 4 * (order // 2) + 2 + order % 2
        close = 4 * ((order + 1) // 2) + (order + 1) % 2
        other = far + (close - far) * ((k - 1) % 2)
        low = (lev % 2 + other % 2) % 2
        high = (lev // 2 % 2 + other // 2 % 2) % 2
        return (lev // 4 + other // 4) % wide * 4 + high * 2 + low

    def near_peer(k):
        return block * NEAR + (mine + k) % NEAR

    def far_peer(k):
        return ((block + k) % blocks) * NEAR + mine

    barrier = pltpu.get_barrier_semaphore()

    @pl.loop(1, levs)
    def _(k):
        pl.semaphore_signal(barrier, inc=1, device_id=(sub, lev_peer(k)), device_id_type=MESH)

    @pl.loop(1, NEAR)
    def _(k):
        pl.semaphore_signal(barrier, inc=1, device_id=(near_peer(k), lev), device_id_type=MESH)

    @pl.loop(1, blocks)
    def _(k):
        pl.semaphore_signal(barrier, inc=1, device_id=(far_peer(k), lev), device_id_type=MESH)

    def weight(half, y):
        return std_ref[pl.ds(half * tall, tall), :] * (1.0 + 0.8 * land_ref[pl.ds(y, 1), :].astype(jnp.float32))

    def natural(half, y):
        return pl.ds(half * tall * rows + y, tall, stride=rows)

    def load_weighted(half, y):
        return field_ref[natural(half, y), :] * weight(half, y)

    def remote(src, dst, send, recv, target):
        return pltpu.make_async_remote_copy(
            src_ref=src, dst_ref=dst, send_sem=send, recv_sem=recv,
            device_id=target, device_id_type=MESH,
        )

    def whole(ref, sem):
        pltpu.make_async_copy(ref, ref, sem).wait()

    def read(ref, half, y):
        return jnp.concatenate([ref[half, v, y] for v in range(HALF)], axis=0)

    def send_levels(half, v):
        def part(peer):
            return slab.at[half, v, pl.ds(peer * share, share)]

        place = gathered.at[half, v, lev]

        @pl.loop(1, levs)
        def _(k):
            peer = lev_peer(k)
            remote(part(peer), place, in_send.at[half, v], in_recv.at[half, v], (sub, peer)).start()

        pltpu.make_async_copy(part(lev), place, in_recv.at[half, v]).start()

    def send_back(half, v):
        def part(peer):
            return mixed.at[half, v, peer]

        place = returned.at[half, v, pl.ds(lev * share, share)]

        @pl.loop(1, levs)
        def _(k):
            peer = lev_peer(k)
            remote(part(peer), place, out_send.at[half, v], out_recv.at[half, v], (sub, peer)).start()

        pltpu.make_async_copy(part(lev), place, out_recv.at[half, v]).start()

    def make_matrix(var):
        modes = modes_ref[var]
        product = lax.dot_general(
            modes * variance_ref[pl.ds(var, 1), :], modes, (((1,), (1,)), ((), ())),
            precision=lax.Precision.HIGHEST, preferred_element_type=jnp.float32,
        )
        high = product.astype(jnp.bfloat16)
        matrix[var, :, : high.shape[1]] = high
        matrix[var, :, high.shape[1] :] = (product - high.astype(jnp.float32)).astype(jnp.bfloat16)

    def mix_levels(half, v):
        whole(gathered.at[half, v], in_recv.at[half, v])
        both = matrix[half * HALF + v]
        high_part = both[:, : both.shape[1] // 2]
        for r in range(share):
            value = gathered[half, v, :, r].reshape(deep, span)
            high = value.astype(jnp.bfloat16)
            low = (value - high.astype(jnp.float32)).astype(jnp.bfloat16)
            product = jnp.dot(
                both, jnp.concatenate([high, high], axis=0), preferred_element_type=jnp.float32
            ) + jnp.dot(high_part, low, preferred_element_type=jnp.float32)
            mixed[half, v, :, r] = product.reshape(levs, deep // levs, span)
        send_back(half, v)

    def doubled(value, steps, y, backward):
        for k in range(doublings):
            shift = span - 2**k if backward else 2**k
            value = value + steps[y, k : k + 1, :] * pltpu.roll(value, shift, 1)
        return value

    def send_near(half, way):
        place = near_in.at[half, way, mine]

        @pl.loop(1, NEAR)
        def _(k):
            remote(
                packed.at[half, way], place, near_send.at[half, way],
                near_recv.at[half, way], (near_peer(k), lev),
            ).start()

        pltpu.make_async_copy(packed.at[half, way], place, near_recv.at[half, way]).start()

    def factor(way, row):
        return mix_ref[pl.ds(way * (2 * NEAR + blocks) + row, 1), :]

    def send_far(half, way):
        whole(near_in.at[half, way], near_recv.at[half, way])
        total = jnp.zeros((tall, span), jnp.float32)
        for j in range(NEAR):
            total = total + factor(way, NEAR + j) * near_in[half, way, j]
        block_sum[half, way] = total
        place = far_in.at[half, way, block]

        @pl.loop(1, blocks)
        def _(k):
            remote(
                block_sum.at[half, way], place, far_send.at[half, way],
                far_recv.at[half, way], (far_peer(k), lev),
            ).start()

        pltpu.make_async_copy(block_sum.at[half, way], place, far_recv.at[half, way]).start()

    def incoming(half, way):
        total = jnp.zeros((tall, span), jnp.float32)
        for j in range(NEAR):
            total = total + factor(way, j) * near_in[half, way, j]
        whole(far_in.at[half, way], far_recv.at[half, way])
        for j in range(blocks):
            total = total + factor(way, 2 * NEAR + j) * far_in[half, way, j]
        return total

    def spread(state, y):
        return jnp.broadcast_to(pltpu.roll(state, (span - y) % span, 1)[:, 0:1], (tall, span))

    def to_slab(half, y, value):
        for v in range(HALF):
            slab[half, v, y] = value[v * 8 : v * 8 + 8]

    together = 16

    def first_sweep(half, load):
        def body(i, pack):
            for u in range(together):
                y = i * together + u
                value = doubled(load(y) * gain_ref[pl.ds(y, 1), :], steps_b_ref, y, True)
                work[half, y] = value
                pack = jnp.where(lanes == y, pltpu.roll(value, y, 1), pack)
            return pack

        packed[half, 0] = lax.fori_loop(
            0, rows // together, body, jnp.zeros((tall, span), jnp.float32)
        )
        send_near(half, 0)

    def second_sweep(half):
        state = incoming(half, 0)
        decay, scaling = cols_ref[0:1, :], cols_ref[1:2, :]

        def down(i, carried):
            for u in range(together):
                y = rows - 1 - (i * together + u)
                entered = work[half, y] + steps_b_ref[y, doublings : doublings + 1, :] * spread(state, y)
                carried = decay * carried + scaling * entered
                work[half, y] = carried
            return carried

        zero = jnp.zeros((tall, span), jnp.float32)
        lax.fori_loop(0, rows // together, down, zero)

        def up(i, both):
            carried, pack = both
            for u in range(together):
                y = i * together + u
                carried = decay * carried + scaling * work[half, y]
                value = doubled(carried * gain_ref[pl.ds(y, 1), :], steps_f_ref, y, False)
                work[half, y] = value
                pack = jnp.where(lanes == y, pltpu.roll(value, y + 1, 1), pack)
            return carried, pack

        packed[half, 1] = lax.fori_loop(0, rows // together, up, (zero, zero))[1]
        send_near(half, 1)

    def last_sweep(half, store):
        state = incoming(half, 1)

        @pl.loop(0, rows // together)
        def _(i):
            for u in range(together):
                y = i * together + u
                store(y, work[half, y] + steps_f_ref[y, doublings : doublings + 1, :] * spread(state, y))

    @pl.loop(0, rows // together)
    def _(i):
        for u in range(together):
            y = i * together + u
            to_slab(0, y, load_weighted(0, y))

    pl.semaphore_wait(barrier, levs + NEAR + blocks - 3)

    for v in range(HALF):
        send_levels(0, v)
    first_sweep(1, lambda y: load_weighted(1, y))

    @pl.loop(0, 2 * HALF)
    def _(var):
        make_matrix(var)

    send_far(1, 0)
    mix_levels(0, 0)
    second_sweep(1)
    mix_levels(0, 1)
    send_far(1, 1)
    mix_levels(0, 2)

    last_sweep(1, lambda y, value: to_slab(1, y, value))
    for v in range(HALF):
        send_levels(1, v)

    for v in range(HALF):
        whole(returned.at[0, v], out_recv.at[0, v])
    first_sweep(0, lambda y: read(returned, 0, y))
    mix_levels(1, 0)
    send_far(0, 0)
    mix_levels(1, 1)
    second_sweep(0)
    mix_levels(1, 2)
    send_far(0, 1)

    def to_output(y, value):
        out_ref[natural(0, y), :] = value * weight(0, y)

    last_sweep(0, to_output)

    for v in range(HALF):
        whole(returned.at[1, v], out_recv.at[1, v])

    @pl.loop(0, rows // together)
    def _(i):
        for u in range(together):
            y = i * together + u
            out_ref[natural(1, y), :] = read(returned, 1, y) * weight(1, y)

    for half in range(2):
        for v in range(HALF):
            sent = gathered.at[half, v, pl.ds(0, levs - 1)]
            whole(sent, in_send.at[half, v])
            whole(sent, out_send.at[half, v])
        for way in range(2):
            whole(near_in.at[half, way, pl.ds(0, NEAR - 1)], near_send.at[half, way])
            whole(far_in.at[half, way, pl.ds(0, blocks - 1)], far_send.at[half, way])


def on_device(
    increment, std_dev, land_mask, row_class, column_class, vertical_modes, mode_variance
):
    variables, levels, rows, span = increment.shape
    subs, levs = lax.axis_size("sub"), lax.axis_size("lev")
    blocks = subs // NEAR
    decay_rows = decay_lookup(row_class, rate_table(span * subs, 1.0 / 24, 1.0 / 40))
    decay_cols = decay_lookup(column_class, rate_table(rows, 1.0 / 8, 1.0 / 12))
    gain_rows = jnp.sqrt(1.0 - decay_rows * decay_rows)
    gain_cols = jnp.sqrt(1.0 - decay_cols * decay_cols)
    steps_b, steps_f, mix = tables_along_x(decay_rows, span, blocks)
    tall = HALF * levels
    deep = levels * levs
    share = rows // levs
    f32 = jnp.float32
    result = pl.pallas_call(
        functools.partial(kernel, subs, levs),
        out_shape=jax.ShapeDtypeStruct((variables * levels * rows, span), f32),
        in_specs=[pl.BlockSpec(memory_space=pltpu.VMEM)] * 10,
        out_specs=pl.BlockSpec(memory_space=pltpu.VMEM),
        scratch_shapes=[
            pltpu.VMEM((2, HALF, rows, levels, span), f32),
            pltpu.VMEM((2, HALF, levs, share, levels, span), f32),
            pltpu.VMEM((2, HALF, levs, share, levels, span), f32),
            pltpu.VMEM((2, HALF, rows, levels, span), f32),
            pltpu.VMEM((2, rows, tall, span), f32),
            pltpu.VMEM((2, 2, tall, span), f32),
            pltpu.VMEM((2, 2, NEAR, tall, span), f32),
            pltpu.VMEM((2, 2, tall, span), f32),
            pltpu.VMEM((2, 2, blocks, tall, span), f32),
            pltpu.VMEM((variables, deep, 2 * deep), jnp.bfloat16),
            pltpu.SemaphoreType.DMA((2, HALF)),
            pltpu.SemaphoreType.DMA((2, HALF)),
            pltpu.SemaphoreType.DMA((2, HALF)),
            pltpu.SemaphoreType.DMA((2, HALF)),
            pltpu.SemaphoreType.DMA((2, 2)),
            pltpu.SemaphoreType.DMA((2, 2)),
            pltpu.SemaphoreType.DMA((2, 2)),
            pltpu.SemaphoreType.DMA((2, 2)),
        ],
        compiler_params=pltpu.CompilerParams(
            collective_id=0, has_side_effects=True, vmem_limit_bytes=40 * 2**20
        ),
    )(
        increment.reshape(variables * levels * rows, span),
        jnp.broadcast_to(std_dev.reshape(variables * levels, 1), (variables * levels, span)),
        land_mask,
        jnp.broadcast_to(gain_rows[:, None], (rows, span)),
        steps_b,
        steps_f,
        mix,
        jnp.stack([decay_cols, gain_cols]),
        vertical_modes,
        mode_variance,
    )
    return result.reshape(increment.shape)


def solution(mesh):
    return jax.shard_map(
        on_device,
        mesh=mesh,
        in_specs=(
            P(None, "lev", None, "sub"),
            P(None, "lev"),
            P(None, "sub"),
            P(),
            P("sub"),
            P(),
            P(),
        ),
        out_specs=P(None, "lev", None, "sub"),
        check_vma=False,
    )
```

```python
import functools

import jax
import jax.numpy as jnp
from jax import lax
from jax.experimental import pallas as pl
from jax.experimental.pallas import tpu as pltpu
from jax.sharding import PartitionSpec as P

MESH = pl.DeviceIdType.MESH
HALF = 3
NEAR = 8


def rate_table(length, fast_one, fast_two):
    return jnp.array(
        [
            fast_one,
            fast_two,
            0.3 / length,
            0.6 / length,
            1.0 / length,
            1.4 / length,
            1.8 / length,
            2.2 / length,
        ],
        jnp.float32,
    )


def decay_lookup(classes, rates):
    matches = classes[:, None] == jnp.arange(8, dtype=jnp.int32)[None, :]
    return jnp.sum(jnp.where(matches, jnp.exp(-rates)[None, :], 0.0), axis=1)


def tables_along_x(decays, span, blocks):
    lane = jnp.arange(span)
    log_decay = jnp.log(decays)
    powers, doubling = decays, []
    for k in range(span.bit_length() - 1):
        doubling.append(powers)
        powers = powers * powers
    offsets = 2 ** jnp.arange(len(doubling))
    doubling = jnp.stack(doubling, axis=1)[:, :, None]
    ahead = (lane[None, :] + offsets[:, None] < span)[None]
    behind = (lane[None, :] >= offsets[:, None])[None]
    entering_b = jnp.exp((span - lane).astype(jnp.float32)[None] * log_decay[:, None])
    entering_f = jnp.exp((lane + 1).astype(jnp.float32)[None] * log_decay[:, None])
    steps_b = jnp.concatenate([jnp.where(ahead, doubling, 0.0), entering_b[:, None]], axis=1)
    steps_f = jnp.concatenate([jnp.where(behind, doubling, 0.0), entering_f[:, None]], axis=1)

    me = lax.axis_index("sub")
    mine, block = me % NEAR, me // NEAR
    near, far = jnp.arange(NEAR), jnp.arange(blocks)

    def power(gap):
        reach = jnp.maximum(gap, 0).astype(jnp.float32) * span
        grown = jnp.exp(reach[:, None] * log_decay[None])
        return jnp.where((gap >= 0)[:, None], grown, 0.0)

    def gated(keep, gap):
        return jnp.where(keep[:, None], power(gap), 0.0)

    mix = jnp.concatenate(
        [
            power(near - mine - 1),
            power(near),
            gated(far > block, NEAR * (far - block - 1) + NEAR - 1 - mine),
            power(mine - near - 1),
            power(NEAR - 1 - near),
            gated(far < block, NEAR * (block - far - 1) + mine),
        ]
    )
    return steps_b, steps_f, jnp.pad(mix, ((0, 0), (0, span - mix.shape[1])))


def kernel(
    subs,
    levs,
    field_ref,
    deviation_ref,
    land_ref,
    gain_ref,
    steps_b_ref,
    steps_f_ref,
    mix_ref,
    cols_ref,
    modes_ref,
    variance_ref,
    out_ref,
    slab,
    gathered,
    mixed,
    returned,
    work,
    packed,
    near_in,
    block_sum,
    far_in,
    matrix,
    std_ref,
    in_send,
    in_recv,
    out_send,
    out_recv,
    near_send,
    near_recv,
    far_send,
    far_recv,
):
    sub, lev = lax.axis_index("sub"), lax.axis_index("lev")
    mine, block = sub % NEAR, sub // NEAR
    blocks = subs // NEAR
    rows = land_ref.shape[0]
    span = land_ref.shape[1]
    share = rows // levs
    tall = work.shape[2]
    deep = matrix.shape[1]
    doublings = span.bit_length() - 1
    lanes = lax.broadcasted_iota(jnp.int32, (tall, span), 1)

    wide = levs // 4

    def lev_peer(k):
        order = (k - 1) // 2
        far = 4 * (order // 2) + 2 + order % 2
        close = 4 * ((order + 1) // 2) + (order + 1) % 2
        other = far + (close - far) * ((k - 1) % 2)
        low = (lev % 2 + other % 2) % 2
        high = (lev // 2 % 2 + other // 2 % 2) % 2
        return (lev // 4 + other // 4) % wide * 4 + high * 2 + low

    def near_peer(k):
        return block * NEAR + (mine + k) % NEAR

    def far_peer(k):
        return ((block + k) % blocks) * NEAR + mine

    barrier = pltpu.get_barrier_semaphore()

    @pl.loop(1, levs)
    def _(k):
        pl.semaphore_signal(barrier, inc=1, device_id=(sub, lev_peer(k)), device_id_type=MESH)

    @pl.loop(1, NEAR)
    def _(k):
        pl.semaphore_signal(barrier, inc=1, device_id=(near_peer(k), lev), device_id_type=MESH)

    @pl.loop(1, blocks)
    def _(k):
        pl.semaphore_signal(barrier, inc=1, device_id=(far_peer(k), lev), device_id_type=MESH)

    eight = deviation_ref.shape[1]
    diagonal = lax.broadcasted_iota(jnp.int32, (eight, eight), 0) == lax.broadcasted_iota(
        jnp.int32, (eight, eight), 1
    )
    for v in range(2 * HALF):
        across = jnp.broadcast_to(deviation_ref[v : v + 1, :], (eight, eight))
        upright = jnp.sum(jnp.where(diagonal, across, 0.0), axis=1, keepdims=True)
        std_ref[v * eight : (v + 1) * eight, :] = jnp.broadcast_to(upright, (eight, span))

    def weight(half, y):
        return std_ref[pl.ds(half * tall, tall), :] * (1.0 + 0.8 * land_ref[pl.ds(y, 1), :].astype(jnp.float32))

    def natural(half, y):
        return pl.ds(half * tall * rows + y, tall, stride=rows)

    def load_weighted(half, y):
        return field_ref[natural(half, y), :] * weight(half, y)

    def remote(src, dst, send, recv, target):
        return pltpu.make_async_remote_copy(
            src_ref=src, dst_ref=dst, send_sem=send, recv_sem=recv,
            device_id=target, device_id_type=MESH,
        )

    def whole(ref, sem):
        pltpu.make_async_copy(ref, ref, sem).wait()

    def read(ref, half, y):
        return jnp.concatenate([ref[half, v, y] for v in range(HALF)], axis=0)

    def send_levels(half, v):
        def part(peer):
            return slab.at[half, v, pl.ds(peer * share, share)]

        place = gathered.at[half, v, lev]

        @pl.loop(1, levs)
        def _(k):
            peer = lev_peer(k)
            remote(part(peer), place, in_send.at[half, v], in_recv.at[half, v], (sub, peer)).start()

        pltpu.make_async_copy(part(lev), place, in_recv.at[half, v]).start()

    def send_back(half, v):
        def part(peer):
            return mixed.at[half, v, peer]

        place = returned.at[half, v, pl.ds(lev * share, share)]

        @pl.loop(1, levs)
        def _(k):
            peer = lev_peer(k)
            remote(part(peer), place, out_send.at[half, v], out_recv.at[half, v], (sub, peer)).start()

        pltpu.make_async_copy(part(lev), place, out_recv.at[half, v]).start()

    def make_matrix(var):
        modes = modes_ref[var]
        product = lax.dot_general(
            modes * variance_ref[pl.ds(var, 1), :], modes, (((1,), (1,)), ((), ())),
            precision=lax.Precision.HIGHEST, preferred_element_type=jnp.float32,
        )
        high = product.astype(jnp.bfloat16)
        matrix[var, :, : high.shape[1]] = high
        matrix[var, :, high.shape[1] :] = (product - high.astype(jnp.float32)).astype(jnp.bfloat16)

    def mix_levels(half, v):
        whole(gathered.at[half, v], in_recv.at[half, v])
        both = matrix[half * HALF + v]
        high_part = both[:, : both.shape[1] // 2]
        for r in range(share):
            value = gathered[half, v, :, r].reshape(deep, span)
            high = value.astype(jnp.bfloat16)
            low = (value - high.astype(jnp.float32)).astype(jnp.bfloat16)
            product = jnp.dot(
                both, jnp.concatenate([high, high], axis=0), preferred_element_type=jnp.float32
            ) + jnp.dot(high_part, low, preferred_element_type=jnp.float32)
            mixed[half, v, :, r] = product.reshape(levs, deep // levs, span)
        send_back(half, v)

    def doubled(value, steps, y, backward):
        for k in range(doublings):
            shift = span - 2**k if backward else 2**k
            value = value + steps[y, k : k + 1, :] * pltpu.roll(value, shift, 1)
        return value

    def send_near(half, way):
        place = near_in.at[half, way, mine]

        @pl.loop(1, NEAR)
        def _(k):
            remote(
                packed.at[half, way], place, near_send.at[half, way],
                near_recv.at[half, way], (near_peer(k), lev),
            ).start()

        pltpu.make_async_copy(packed.at[half, way], place, near_recv.at[half, way]).start()

    def factor(way, row):
        return mix_ref[pl.ds(way * (2 * NEAR + blocks) + row, 1), :]

    def send_far(half, way):
        whole(near_in.at[half, way], near_recv.at[half, way])
        total = jnp.zeros((tall, span), jnp.float32)
        for j in range(NEAR):
            total = total + factor(way, NEAR + j) * near_in[half, way, j]
        block_sum[half, way] = total
        place = far_in.at[half, way, block]

        @pl.loop(1, blocks)
        def _(k):
            remote(
                block_sum.at[half, way], place, far_send.at[half, way],
                far_recv.at[half, way], (far_peer(k), lev),
            ).start()

        pltpu.make_async_copy(block_sum.at[half, way], place, far_recv.at[half, way]).start()

    def incoming(half, way):
        total = jnp.zeros((tall, span), jnp.float32)
        for j in range(NEAR):
            total = total + factor(way, j) * near_in[half, way, j]
        whole(far_in.at[half, way], far_recv.at[half, way])
        for j in range(blocks):
            total = total + factor(way, 2 * NEAR + j) * far_in[half, way, j]
        return total

    def spread(state, y):
        return jnp.broadcast_to(pltpu.roll(state, (span - y) % span, 1)[:, 0:1], (tall, span))

    def to_slab(half, y, value):
        for v in range(HALF):
            slab[half, v, y] = value[v * 8 : v * 8 + 8]

    together = 16

    def first_sweep(half, load):
        def body(i, pack):
            for u in range(together):
                y = i * together + u
                value = doubled(load(y) * gain_ref[pl.ds(y, 1), :], steps_b_ref, y, True)
                work[half, y] = value
                pack = jnp.where(lanes == y, pltpu.roll(value, y, 1), pack)
            return pack

        packed[half, 0] = lax.fori_loop(
            0, rows // together, body, jnp.zeros((tall, span), jnp.float32)
        )

    def second_sweep(half):
        state = incoming(half, 0)
        decay, scaling = cols_ref[0:1, :], cols_ref[1:2, :]

        def down(i, carried):
            for u in range(together):
                y = rows - 1 - (i * together + u)
                entered = work[half, y] + steps_b_ref[y, doublings : doublings + 1, :] * spread(state, y)
                carried = decay * carried + scaling * entered
                work[half, y] = carried
            return carried

        zero = jnp.zeros((tall, span), jnp.float32)
        lax.fori_loop(0, rows // together, down, zero)

        def up(i, both):
            carried, pack = both
            for u in range(together):
                y = i * together + u
                carried = decay * carried + scaling * work[half, y]
                value = doubled(carried * gain_ref[pl.ds(y, 1), :], steps_f_ref, y, False)
                work[half, y] = value
                pack = jnp.where(lanes == y, pltpu.roll(value, y + 1, 1), pack)
            return carried, pack

        packed[half, 1] = lax.fori_loop(0, rows // together, up, (zero, zero))[1]
        send_near(half, 1)

    def last_sweep(half, store):
        state = incoming(half, 1)

        @pl.loop(0, rows // together)
        def _(i):
            for u in range(together):
                y = i * together + u
                store(y, work[half, y] + steps_f_ref[y, doublings : doublings + 1, :] * spread(state, y))

    @pl.loop(0, rows // together)
    def _(i):
        for u in range(together):
            y = i * together + u
            to_slab(0, y, load_weighted(0, y))

    first_sweep(1, lambda y: load_weighted(1, y))
    pl.semaphore_wait(barrier, levs + NEAR + blocks - 3)

    send_near(1, 0)
    send_levels(0, 0)
    send_far(1, 0)
    send_levels(0, 1)
    send_levels(0, 2)

    @pl.loop(0, 2 * HALF)
    def _(var):
        make_matrix(var)

    mix_levels(0, 0)
    second_sweep(1)
    send_far(1, 1)
    mix_levels(0, 1)
    mix_levels(0, 2)
    last_sweep(1, lambda y, value: to_slab(1, y, value))

    send_levels(1, 0)
    for v in range(HALF):
        whole(returned.at[0, v], out_recv.at[0, v])
    first_sweep(0, lambda y: read(returned, 0, y))
    send_near(0, 0)
    send_far(0, 0)
    send_levels(1, 1)
    send_levels(1, 2)
    mix_levels(1, 0)
    second_sweep(0)
    send_far(0, 1)
    mix_levels(1, 1)
    mix_levels(1, 2)

    def to_output(y, value):
        out_ref[natural(0, y), :] = value * weight(0, y)

    last_sweep(0, to_output)

    for v in range(HALF):
        whole(returned.at[1, v], out_recv.at[1, v])

    @pl.loop(0, rows // together)
    def _(i):
        for u in range(together):
            y = i * together + u
            out_ref[natural(1, y), :] = read(returned, 1, y) * weight(1, y)

    for half in range(2):
        for v in range(HALF):
            sent = gathered.at[half, v, pl.ds(0, levs - 1)]
            whole(sent, in_send.at[half, v])
            whole(sent, out_send.at[half, v])
        for way in range(2):
            whole(near_in.at[half, way, pl.ds(0, NEAR - 1)], near_send.at[half, way])
            whole(far_in.at[half, way, pl.ds(0, blocks - 1)], far_send.at[half, way])


def on_device(
    increment, std_dev, land_mask, row_class, column_class, vertical_modes, mode_variance
):
    variables, levels, rows, span = increment.shape
    subs, levs = lax.axis_size("sub"), lax.axis_size("lev")
    blocks = subs // NEAR
    decay_rows = decay_lookup(row_class, rate_table(span * subs, 1.0 / 24, 1.0 / 40))
    decay_cols = decay_lookup(column_class, rate_table(rows, 1.0 / 8, 1.0 / 12))
    gain_rows = jnp.sqrt(1.0 - decay_rows * decay_rows)
    gain_cols = jnp.sqrt(1.0 - decay_cols * decay_cols)
    steps_b, steps_f, mix = tables_along_x(decay_rows, span, blocks)
    tall = HALF * levels
    deep = levels * levs
    share = rows // levs
    f32 = jnp.float32
    result = pl.pallas_call(
        functools.partial(kernel, subs, levs),
        out_shape=jax.ShapeDtypeStruct((variables * levels * rows, span), f32),
        in_specs=[pl.BlockSpec(memory_space=pltpu.VMEM)] * 10,
        out_specs=pl.BlockSpec(memory_space=pltpu.VMEM),
        scratch_shapes=[
            pltpu.VMEM((2, HALF, rows, levels, span), f32),
            pltpu.VMEM((2, HALF, levs, share, levels, span), f32),
            pltpu.VMEM((2, HALF, levs, share, levels, span), f32),
            pltpu.VMEM((2, HALF, rows, levels, span), f32),
            pltpu.VMEM((2, rows, tall, span), f32),
            pltpu.VMEM((2, 2, tall, span), f32),
            pltpu.VMEM((2, 2, NEAR, tall, span), f32),
            pltpu.VMEM((2, 2, tall, span), f32),
            pltpu.VMEM((2, 2, blocks, tall, span), f32),
            pltpu.VMEM((variables, deep, 2 * deep), jnp.bfloat16),
            pltpu.VMEM((variables * levels, span), f32),
            pltpu.SemaphoreType.DMA((2, HALF)),
            pltpu.SemaphoreType.DMA((2, HALF)),
            pltpu.SemaphoreType.DMA((2, HALF)),
            pltpu.SemaphoreType.DMA((2, HALF)),
            pltpu.SemaphoreType.DMA((2, 2)),
            pltpu.SemaphoreType.DMA((2, 2)),
            pltpu.SemaphoreType.DMA((2, 2)),
            pltpu.SemaphoreType.DMA((2, 2)),
        ],
        compiler_params=pltpu.CompilerParams(
            collective_id=0, has_side_effects=True, vmem_limit_bytes=40 * 2**20
        ),
    )(
        increment.reshape(variables * levels * rows, span),
        std_dev,
        land_mask,
        jnp.broadcast_to(gain_rows[:, None], (rows, span)),
        steps_b,
        steps_f,
        mix,
        jnp.stack([decay_cols, gain_cols]),
        vertical_modes,
        mode_variance,
    )
    return result.reshape(increment.shape)


def solution(mesh):
    return jax.shard_map(
        on_device,
        mesh=mesh,
        in_specs=(
            P(None, "lev", None, "sub"),
            P(None, "lev"),
            P(None, "sub"),
            P(),
            P("sub"),
            P(),
            P(),
        ),
        out_specs=P(None, "lev", None, "sub"),
        check_vma=False,
    )
```

```python
import functools

import jax
import jax.numpy as jnp
from jax import lax
from jax.experimental import pallas as pl
from jax.experimental.pallas import tpu as pltpu
from jax.sharding import PartitionSpec as P

MESH = pl.DeviceIdType.MESH
HALF = 3
NEAR = 8


def rate_table(length, fast_one, fast_two):
    return jnp.array(
        [
            fast_one,
            fast_two,
            0.3 / length,
            0.6 / length,
            1.0 / length,
            1.4 / length,
            1.8 / length,
            2.2 / length,
        ],
        jnp.float32,
    )


def decay_lookup(classes, rates):
    matches = classes[:, None] == jnp.arange(8, dtype=jnp.int32)[None, :]
    return jnp.sum(jnp.where(matches, jnp.exp(-rates)[None, :], 0.0), axis=1)


def tables_along_x(decays, span, blocks):
    lane = jnp.arange(span)
    log_decay = jnp.log(decays)
    powers, doubling = decays, []
    for k in range(span.bit_length() - 1):
        doubling.append(powers)
        powers = powers * powers
    offsets = 2 ** jnp.arange(len(doubling))
    doubling = jnp.stack(doubling, axis=1)[:, :, None]
    ahead = (lane[None, :] + offsets[:, None] < span)[None]
    behind = (lane[None, :] >= offsets[:, None])[None]
    entering_b = jnp.exp((span - lane).astype(jnp.float32)[None] * log_decay[:, None])
    entering_f = jnp.exp((lane + 1).astype(jnp.float32)[None] * log_decay[:, None])
    steps_b = jnp.concatenate([jnp.where(ahead, doubling, 0.0), entering_b[:, None]], axis=1)
    steps_f = jnp.concatenate([jnp.where(behind, doubling, 0.0), entering_f[:, None]], axis=1)

    me = lax.axis_index("sub")
    mine, block = me % NEAR, me // NEAR
    near, far = jnp.arange(NEAR), jnp.arange(blocks)

    def power(gap):
        reach = jnp.maximum(gap, 0).astype(jnp.float32) * span
        grown = jnp.exp(reach[:, None] * log_decay[None])
        return jnp.where((gap >= 0)[:, None], grown, 0.0)

    def gated(keep, gap):
        return jnp.where(keep[:, None], power(gap), 0.0)

    mix = jnp.concatenate(
        [
            power(near - mine - 1),
            power(near),
            gated(far > block, NEAR * (far - block - 1) + NEAR - 1 - mine),
            power(mine - near - 1),
            power(NEAR - 1 - near),
            gated(far < block, NEAR * (block - far - 1) + mine),
        ]
    )
    return steps_b, steps_f, jnp.pad(mix, ((0, 0), (0, span - mix.shape[1])))


def kernel(
    subs,
    levs,
    field_ref,
    deviation_ref,
    land_ref,
    gain_ref,
    steps_b_ref,
    steps_f_ref,
    mix_ref,
    cols_ref,
    modes_ref,
    variance_ref,
    out_ref,
    slab,
    gathered,
    mixed,
    returned,
    work,
    packed,
    near_in,
    block_sum,
    far_in,
    matrix,
    std_ref,
    in_send,
    in_recv,
    out_send,
    out_recv,
    near_send,
    near_recv,
    far_send,
    far_recv,
):
    sub, lev = lax.axis_index("sub"), lax.axis_index("lev")
    mine, block = sub % NEAR, sub // NEAR
    blocks = subs // NEAR
    rows = land_ref.shape[0]
    span = land_ref.shape[1]
    share = rows // levs
    tall = work.shape[2]
    deep = matrix.shape[1]
    doublings = span.bit_length() - 1
    lanes = lax.broadcasted_iota(jnp.int32, (tall, span), 1)

    wide = levs // 4

    def lev_peer(k):
        order = (k - 1) // 2
        far = 4 * (order // 2) + 2 + order % 2
        close = 4 * ((order + 1) // 2) + (order + 1) % 2
        other = far + (close - far) * ((k - 1) % 2)
        low = (lev % 2 + other % 2) % 2
        high = (lev // 2 % 2 + other // 2 % 2) % 2
        return (lev // 4 + other // 4) % wide * 4 + high * 2 + low

    def near_peer(k):
        return block * NEAR + (mine + k) % NEAR

    def far_peer(k):
        return ((block + k) % blocks) * NEAR + mine

    barrier = pltpu.get_barrier_semaphore()

    @pl.loop(1, levs)
    def _(k):
        pl.semaphore_signal(barrier, inc=1, device_id=(sub, lev_peer(k)), device_id_type=MESH)

    @pl.loop(1, NEAR)
    def _(k):
        pl.semaphore_signal(barrier, inc=1, device_id=(near_peer(k), lev), device_id_type=MESH)

    @pl.loop(1, blocks)
    def _(k):
        pl.semaphore_signal(barrier, inc=1, device_id=(far_peer(k), lev), device_id_type=MESH)

    eight = deviation_ref.shape[1]
    diagonal = lax.broadcasted_iota(jnp.int32, (eight, eight), 0) == lax.broadcasted_iota(
        jnp.int32, (eight, eight), 1
    )
    for v in range(2 * HALF):
        across = jnp.broadcast_to(deviation_ref[v : v + 1, :], (eight, eight))
        upright = jnp.sum(jnp.where(diagonal, across, 0.0), axis=1, keepdims=True)
        std_ref[v * eight : (v + 1) * eight, :] = jnp.broadcast_to(upright, (eight, span))

    def weight(half, y):
        return std_ref[pl.ds(half * tall, tall), :] * (1.0 + 0.8 * land_ref[pl.ds(y, 1), :].astype(jnp.float32))

    def natural(half, y):
        return pl.ds(half * tall * rows + y, tall, stride=rows)

    def load_weighted(half, y):
        return field_ref[natural(half, y), :] * weight(half, y)

    def remote(src, dst, send, recv, target):
        return pltpu.make_async_remote_copy(
            src_ref=src, dst_ref=dst, send_sem=send, recv_sem=recv,
            device_id=target, device_id_type=MESH,
        )

    def whole(ref, sem):
        pltpu.make_async_copy(ref, ref, sem).wait()

    def read(ref, half, y):
        return jnp.concatenate([ref[half, v, y] for v in range(HALF)], axis=0)

    def send_levels(half, v):
        def part(peer):
            return slab.at[half, v, pl.ds(peer * share, share)]

        place = gathered.at[half, v, lev]

        @pl.loop(1, levs)
        def _(k):
            peer = lev_peer(k)
            remote(part(peer), place, in_send.at[half, v], in_recv.at[half, v], (sub, peer)).start()

        pltpu.make_async_copy(part(lev), place, in_recv.at[half, v]).start()

    def send_back(half, v):
        def part(peer):
            return mixed.at[half, v, peer]

        place = returned.at[half, v, pl.ds(lev * share, share)]

        @pl.loop(1, levs)
        def _(k):
            peer = lev_peer(k)
            remote(part(peer), place, out_send.at[half, v], out_recv.at[half, v], (sub, peer)).start()

        pltpu.make_async_copy(part(lev), place, out_recv.at[half, v]).start()

    def make_matrix(var):
        modes = modes_ref[var]
        product = lax.dot_general(
            modes * variance_ref[pl.ds(var, 1), :], modes, (((1,), (1,)), ((), ())),
            precision=lax.Precision.HIGHEST, preferred_element_type=jnp.float32,
        )
        high = product.astype(jnp.bfloat16)
        matrix[var, :, : high.shape[1]] = high
        matrix[var, :, high.shape[1] :] = (product - high.astype(jnp.float32)).astype(jnp.bfloat16)

    def mix_levels(half, v):
        whole(gathered.at[half, v], in_recv.at[half, v])
        both = matrix[half * HALF + v]
        high_part = both[:, : both.shape[1] // 2]
        for r in range(share):
            value = gathered[half, v, :, r].reshape(deep, span)
            high = value.astype(jnp.bfloat16)
            low = (value - high.astype(jnp.float32)).astype(jnp.bfloat16)
            product = jnp.dot(
                both, jnp.concatenate([high, high], axis=0), preferred_element_type=jnp.float32
            ) + jnp.dot(high_part, low, preferred_element_type=jnp.float32)
            mixed[half, v, :, r] = product.reshape(levs, deep // levs, span)
        send_back(half, v)

    def doubled(value, steps, y, backward):
        for k in range(doublings):
            shift = span - 2**k if backward else 2**k
            value = value + steps[y, k : k + 1, :] * pltpu.roll(value, shift, 1)
        return value

    def send_near(half, way):
        place = near_in.at[half, way, mine]

        @pl.loop(1, NEAR)
        def _(k):
            remote(
                packed.at[half, way], place, near_send.at[half, way],
                near_recv.at[half, way], (near_peer(k), lev),
            ).start()

        pltpu.make_async_copy(packed.at[half, way], place, near_recv.at[half, way]).start()

    def factor(way, row):
        return mix_ref[pl.ds(way * (2 * NEAR + blocks) + row, 1), :]

    def send_far(half, way):
        whole(near_in.at[half, way], near_recv.at[half, way])
        total = jnp.zeros((tall, span), jnp.float32)
        for j in range(NEAR):
            total = total + factor(way, NEAR + j) * near_in[half, way, j]
        block_sum[half, way, 0:8] = total[0:8] + pltpu.roll(total[8:16], span // 2, 1)
        block_sum[half, way, 8:16] = total[16:24]
        place = far_in.at[half, way, block]

        @pl.loop(1, blocks)
        def _(k):
            remote(
                block_sum.at[half, way], place, far_send.at[half, way],
                far_recv.at[half, way], (far_peer(k), lev),
            ).start()

        pltpu.make_async_copy(block_sum.at[half, way], place, far_recv.at[half, way]).start()

    def incoming(half, way):
        total = jnp.zeros((tall, span), jnp.float32)
        for j in range(NEAR):
            total = total + factor(way, j) * near_in[half, way, j]
        whole(far_in.at[half, way], far_recv.at[half, way])
        for j in range(blocks):
            shared = far_in[half, way, j, 0:8]
            state = jnp.concatenate(
                [shared, pltpu.roll(shared, span // 2, 1), far_in[half, way, j, 8:16]], axis=0
            )
            total = total + factor(way, 2 * NEAR + j) * state
        return total

    def spread(state, y):
        return jnp.broadcast_to(pltpu.roll(state, (span - y) % span, 1)[:, 0:1], (tall, span))

    def to_slab(half, y, value):
        for v in range(HALF):
            slab[half, v, y] = value[v * 8 : v * 8 + 8]

    together = 16

    def first_sweep(half, load):
        def body(i, pack):
            for u in range(together):
                y = i * together + u
                value = doubled(load(y) * gain_ref[pl.ds(y, 1), :], steps_b_ref, y, True)
                work[half, y] = value
                pack = jnp.where(lanes == y, pltpu.roll(value, y, 1), pack)
            return pack

        packed[half, 0] = lax.fori_loop(
            0, rows // together, body, jnp.zeros((tall, span), jnp.float32)
        )

    def second_sweep(half):
        state = incoming(half, 0)
        decay, scaling = cols_ref[0:1, :], cols_ref[1:2, :]

        def down(i, carried):
            for u in range(together):
                y = rows - 1 - (i * together + u)
                entered = work[half, y] + steps_b_ref[y, doublings : doublings + 1, :] * spread(state, y)
                carried = decay * carried + scaling * entered
                work[half, y] = carried
            return carried

        zero = jnp.zeros((tall, span), jnp.float32)
        lax.fori_loop(0, rows // together, down, zero)

        def up(i, both):
            carried, pack = both
            for u in range(together):
                y = i * together + u
                carried = decay * carried + scaling * work[half, y]
                value = doubled(carried * gain_ref[pl.ds(y, 1), :], steps_f_ref, y, False)
                work[half, y] = value
                pack = jnp.where(lanes == y, pltpu.roll(value, y + 1, 1), pack)
            return carried, pack

        packed[half, 1] = lax.fori_loop(0, rows // together, up, (zero, zero))[1]
        send_near(half, 1)

    def last_sweep(half, store):
        state = incoming(half, 1)

        @pl.loop(0, rows // together)
        def _(i):
            for u in range(together):
                y = i * together + u
                store(y, work[half, y] + steps_f_ref[y, doublings : doublings + 1, :] * spread(state, y))

    @pl.loop(0, rows // together)
    def _(i):
        for u in range(together):
            y = i * together + u
            to_slab(0, y, load_weighted(0, y))

    first_sweep(1, lambda y: load_weighted(1, y))
    pl.semaphore_wait(barrier, levs + NEAR + blocks - 3)

    send_near(1, 0)
    send_levels(0, 0)
    send_far(1, 0)
    send_levels(0, 1)
    send_levels(0, 2)

    @pl.loop(0, 2 * HALF)
    def _(var):
        make_matrix(var)

    mix_levels(0, 0)
    second_sweep(1)
    send_far(1, 1)
    mix_levels(0, 1)
    mix_levels(0, 2)
    last_sweep(1, lambda y, value: to_slab(1, y, value))

    send_levels(1, 0)
    for v in range(HALF):
        whole(returned.at[0, v], out_recv.at[0, v])
    first_sweep(0, lambda y: read(returned, 0, y))
    send_near(0, 0)
    send_far(0, 0)
    send_levels(1, 1)
    send_levels(1, 2)
    mix_levels(1, 0)
    second_sweep(0)
    send_far(0, 1)
    mix_levels(1, 1)
    mix_levels(1, 2)

    def to_output(y, value):
        out_ref[natural(0, y), :] = value * weight(0, y)

    last_sweep(0, to_output)

    for v in range(HALF):
        whole(returned.at[1, v], out_recv.at[1, v])

    @pl.loop(0, rows // together)
    def _(i):
        for u in range(together):
            y = i * together + u
            out_ref[natural(1, y), :] = read(returned, 1, y) * weight(1, y)

    for half in range(2):
        for v in range(HALF):
            sent = gathered.at[half, v, pl.ds(0, levs - 1)]
            whole(sent, in_send.at[half, v])
            whole(sent, out_send.at[half, v])
        for way in range(2):
            whole(near_in.at[half, way, pl.ds(0, NEAR - 1)], near_send.at[half, way])
            whole(far_in.at[half, way, pl.ds(0, blocks - 1)], far_send.at[half, way])


def on_device(
    increment, std_dev, land_mask, row_class, column_class, vertical_modes, mode_variance
):
    variables, levels, rows, span = increment.shape
    subs, levs = lax.axis_size("sub"), lax.axis_size("lev")
    blocks = subs // NEAR
    decay_rows = decay_lookup(row_class, rate_table(span * subs, 1.0 / 24, 1.0 / 40))
    decay_cols = decay_lookup(column_class, rate_table(rows, 1.0 / 8, 1.0 / 12))
    gain_rows = jnp.sqrt(1.0 - decay_rows * decay_rows)
    gain_cols = jnp.sqrt(1.0 - decay_cols * decay_cols)
    steps_b, steps_f, mix = tables_along_x(decay_rows, span, blocks)
    tall = HALF * levels
    deep = levels * levs
    share = rows // levs
    f32 = jnp.float32
    result = pl.pallas_call(
        functools.partial(kernel, subs, levs),
        out_shape=jax.ShapeDtypeStruct((variables * levels * rows, span), f32),
        in_specs=[pl.BlockSpec(memory_space=pltpu.VMEM)] * 10,
        out_specs=pl.BlockSpec(memory_space=pltpu.VMEM),
        scratch_shapes=[
            pltpu.VMEM((2, HALF, rows, levels, span), f32),
            pltpu.VMEM((2, HALF, levs, share, levels, span), f32),
            pltpu.VMEM((2, HALF, levs, share, levels, span), f32),
            pltpu.VMEM((2, HALF, rows, levels, span), f32),
            pltpu.VMEM((2, rows, tall, span), f32),
            pltpu.VMEM((2, 2, tall, span), f32),
            pltpu.VMEM((2, 2, NEAR, tall, span), f32),
            pltpu.VMEM((2, 2, 2 * levels, span), f32),
            pltpu.VMEM((2, 2, blocks, 2 * levels, span), f32),
            pltpu.VMEM((variables, deep, 2 * deep), jnp.bfloat16),
            pltpu.VMEM((variables * levels, span), f32),
            pltpu.SemaphoreType.DMA((2, HALF)),
            pltpu.SemaphoreType.DMA((2, HALF)),
            pltpu.SemaphoreType.DMA((2, HALF)),
            pltpu.SemaphoreType.DMA((2, HALF)),
            pltpu.SemaphoreType.DMA((2, 2)),
            pltpu.SemaphoreType.DMA((2, 2)),
            pltpu.SemaphoreType.DMA((2, 2)),
            pltpu.SemaphoreType.DMA((2, 2)),
        ],
        compiler_params=pltpu.CompilerParams(
            collective_id=0, has_side_effects=True, vmem_limit_bytes=40 * 2**20
        ),
    )(
        increment.reshape(variables * levels * rows, span),
        std_dev,
        land_mask,
        jnp.broadcast_to(gain_rows[:, None], (rows, span)),
        steps_b,
        steps_f,
        mix,
        jnp.stack([decay_cols, gain_cols]),
        vertical_modes,
        mode_variance,
    )
    return result.reshape(increment.shape)


def solution(mesh):
    return jax.shard_map(
        on_device,
        mesh=mesh,
        in_specs=(
            P(None, "lev", None, "sub"),
            P(None, "lev"),
            P(None, "sub"),
            P(),
            P("sub"),
            P(),
            P(),
        ),
        out_specs=P(None, "lev", None, "sub"),
        check_vma=False,
    )
```
